512 devices in a mesh: wide: 128 (over z, x, core), narrow: 4 (over y).
Axes of the slice: x: 4, y: 4, z: 16, core: 2. Of those that a mesh axis runs over, the one named last changes fastest.
Arguments:
- totals: float32 [16, 4096, 512], P('narrow', 'wide'), may hold values from 0.5 to 2
- courant: float32 [4096, 512], P('wide'), may hold values from 0.05 to 0.4
- diffusion: float32 [4096, 512], P('wide'), may hold values from 0.02 to 0.14
- stoich: float32 [32, 16], replicated, may hold values from 0 to 0.5
- log_k: float32 [32], replicated, may hold values from -2 to 0
- mineral_stoich: float32 [12, 16], replicated, may hold values from 0 to 0.5
- mineral_log_k: float32 [12], replicated, may hold values from 0 to 2
- mineral_rate: float32 [12], replicated, may hold values from 0.05 to 1
- front_counts: int32 [128, 4], replicated, may hold values from 0 to 16, as said below
- mineral_flags: int32 [2048, 4], P('wide', 'narrow'), may hold values 0 or 1
Outputs:
- speciated: float32 [16, 4096, 512], P(None, 'wide', 'narrow')
The draws below stay inside these ranges and needn't reach their ends.
Inputs may be any that keep to these rules, and one draw needn't show every extreme that they name: `front_counts`: some tile has all 16 of its blocks front.
All inputs are finite; a program needn't handle non-finite values. Where the reference program divides by a largest or mean magnitude, that divisor is 1e-20 or more. No bound on the sum of `mineral_flags` on one device may be relied on, other than what follows from the above.
Results may differ from the reference program's by a relative error of at most 0.0003.
Values sent between devices are 32-bit elements; how exact they have to be, the bound alone decides.
No kernel may reach another device: no remote copies, remote signals or barrier semaphores. Data moves between devices by JAX's collectives and lax.ppermute only.
A program may use at most 64 MiB of HBM per device.

```python
import math
import jax
import jax.numpy as jnp
from jax import lax

NC = 16
NM = 12
NSEC = 32
CX = 32
YT = 128
STEPS = 4
ITERS = 4
NBLK = 16
NX = 4096
NY = 512
N_NARROW = 4


def draw_front_counts(key, part):
    tiles_x = NX // CX
    tiles_y = NY // YT
    key_light, key_busy, key_full = jax.random.split(key, 3)
    light_load = jax.random.randint(key_light, (tiles_x, tiles_y), 0, NBLK // 4 + 1)
    busy_tile = jax.random.randint(key_busy, (tiles_x, tiles_y), 0, 8) == 0
    counts = jnp.where(busy_tile, NBLK, light_load).reshape(-1)
    chosen = jax.random.randint(key_full, (), 0, tiles_x * tiles_y)
    counts = counts.at[chosen].set(NBLK)
    return counts.reshape(tiles_x, tiles_y).astype(jnp.int32)


def place_ends(values, rng, low, high):
    place = [jax.random.randint(jax.random.fold_in(rng, axis), (), 0, length) for axis, length in enumerate(values.shape)]
    main_axis = values.shape.index(max(values.shape))
    next_to = place[:main_axis] + [(place[main_axis] + 1) % values.shape[main_axis]] + place[main_axis + 1:]
    return values.at[tuple(place)].set(low).at[tuple(next_to)].set(high)


def level_of(own_key, extent, cuts, least, high):
    def one(dim, blocks):
        draws = jax.random.uniform(jax.random.fold_in(jax.random.fold_in(own_key, 6), dim), (blocks,), jnp.float32, least / len(cuts), high / len(cuts))
        return jnp.repeat(jnp.exp(draws), extent[dim] // blocks).reshape((-1,) + (1,) * (len(extent) - dim - 1))

    level = one(*cuts[0])
    for cut in cuts[1:]:
        level = level * one(*cut)
    return level


def setup_inputs(seed: int = 0) -> dict:
    streams_of = jax.random.split(jax.random.key(seed), 11)
    totals = jnp.clip(0.5 + 1.5 * jax.random.uniform(streams_of[0], (NC, NX, NY), jnp.float32) ** level_of(streams_of[0], (NC, NX, NY), ((0, 4), (1, 128)), -0.2, 0.2), 0.5, 2.0)
    courant = jnp.clip(0.05 + 0.35 * jax.random.uniform(streams_of[1], (NX, NY), jnp.float32) ** level_of(streams_of[1], (NX, NY), ((0, 128),), -0.2, 0.2), 0.05, 0.4)
    diffusion = jnp.clip(0.02 + 0.12000000104308128 * jax.random.uniform(streams_of[2], (NX, NY), jnp.float32) ** level_of(streams_of[2], (NX, NY), ((0, 128),), -0.2, 0.2), 0.02, 0.14)
    stoich = jnp.clip(jax.random.uniform(streams_of[3], (NSEC, NC), jnp.float32, 0.0, 0.5), 0.0, 0.5)
    log_k = jnp.clip(jax.random.uniform(streams_of[4], (NSEC,), jnp.float32, -2.0, 0.0), -2.0, 0.0)
    mineral_stoich = jnp.clip(jax.random.uniform(streams_of[5], (NM, NC), jnp.float32, 0.0, 0.5), 0.0, 0.5)
    mineral_log_k = jnp.clip(jax.random.uniform(streams_of[6], (NM,), jnp.float32, 0.0, 2.0), 0.0, 2.0)
    mineral_rate = jnp.clip(jnp.exp(jax.random.uniform(streams_of[7], (NM,), jnp.float32, math.log(0.05), math.log(1.0))), 0.05, 1.0)
    front_counts = draw_front_counts(jax.random.fold_in(streams_of[10], 71), 0)
    mineral_flags = place_ends((jax.random.randint(streams_of[9], (NX // 2, N_NARROW), 0, 2) < 1).astype(jnp.int32), jax.random.fold_in(streams_of[9], 1), 0, 1)
    return {"totals": totals, "courant": courant, "diffusion": diffusion, "stoich": stoich, "log_k": log_k, "mineral_stoich": mineral_stoich, "mineral_log_k": mineral_log_k, "mineral_rate": mineral_rate, "front_counts": front_counts, "mineral_flags": mineral_flags}


def advance(fields, upwind, downwind, courant, diffusion):
    beside = jnp.pad(fields, ((0, 0), (0, 0), (1, 1)))
    return fields - courant * (fields - upwind) + diffusion * ((upwind + downwind) + (beside[:, :, :-2] + beside[:, :, 2:]) - 4.0 * fields)


def pair_table(matrix):
    return (matrix[:, :, None] * matrix[:, None, :]).reshape(matrix.shape[0], -1).T


def solve_batch(jacobian, residual):
    order = residual.shape[0]
    matrix_rows = [jacobian[i] for i in range(order)]
    values = [residual[i] for i in range(order)]
    for pivot_index in range(order):
        pivot_row = matrix_rows[pivot_index]
        for target in range(pivot_index + 1, order):
            factor = matrix_rows[target][pivot_index] / pivot_row[pivot_index]
            matrix_rows[target] = matrix_rows[target] - factor[None, :] * pivot_row
            values[target] = values[target] - factor * values[pivot_index]
    solution = [None] * order
    for pivot_index in reversed(range(order)):
        partial_sum = values[pivot_index]
        for column in range(pivot_index + 1, order):
            partial_sum = partial_sum - matrix_rows[pivot_index][column] * solution[column]
        solution[pivot_index] = partial_sum / matrix_rows[pivot_index][pivot_index]
    return jnp.stack(solution)


def speciate(total, mineral_on, stoich, log_k, mineral_stoich, mineral_log_k, mineral_rate, pair_sec, pair_min):
    highest = lax.Precision.HIGHEST
    order = total.shape[0]
    free_log = jnp.log(total)
    for repeat in range(ITERS):
        free_conc = jnp.exp(free_log)
        secondary = jnp.exp(log_k[:, None] + jnp.dot(stoich, free_log, precision=highest))
        saturation = mineral_rate[:, None] * jnp.exp(jnp.dot(mineral_stoich, free_log, precision=highest) - mineral_log_k[:, None])
        residual = free_conc + jnp.dot(stoich.T, secondary, precision=highest) + mineral_on * jnp.dot(mineral_stoich.T, saturation, precision=highest) - total
        jacobian = jnp.dot(pair_sec, secondary, precision=highest) + mineral_on * jnp.dot(pair_min, saturation, precision=highest)
        jacobian = jacobian.reshape(order, order, -1) + jnp.eye(order, dtype=jnp.float32)[:, :, None] * free_conc[:, None, :]
        newton_step = solve_batch(jacobian, residual)
        largest = jnp.max(jnp.abs(newton_step), axis=0)
        free_log = free_log - newton_step / jnp.maximum(largest, 1.0)
    return free_log


def reference(totals, courant, diffusion, stoich, log_k, mineral_stoich, mineral_log_k, mineral_rate, front_counts, mineral_flags):
    fields = totals
    for repeat in range(STEPS):
        padded = jnp.pad(fields, ((0, 0), (1, 1), (0, 0)))
        fields = advance(fields, padded[:, :-2], padded[:, 2:], courant, diffusion)
    pair_sec = pair_table(stoich)
    pair_min = pair_table(mineral_stoich)
    tiles_y = NY // YT

    def one_pair(row_pair):
        rows_here = lax.dynamic_slice_in_dim(fields, row_pair * 2, 2, 1)
        blocks = rows_here.reshape(NC, 2, tiles_y, YT).transpose(2, 0, 1, 3).reshape(tiles_y, NC, 2 * YT)
        flag_row = mineral_flags[row_pair].astype(jnp.float32)
        solved = jax.vmap(lambda block, mineral_on: speciate(block, mineral_on, stoich, log_k, mineral_stoich, mineral_log_k, mineral_rate, pair_sec, pair_min))(blocks, flag_row)
        is_front = (row_pair % NBLK) < front_counts[row_pair // NBLK]
        chosen = jnp.where(is_front[:, None, None], solved, jnp.log(blocks))
        return chosen.reshape(tiles_y, NC, 2, YT).transpose(1, 2, 0, 3).reshape(NC, 2, NY)

    speciated = lax.map(one_pair, jnp.arange(NX // 2, dtype=jnp.int32))
    return speciated.transpose(1, 0, 2, 3).reshape(NC, NX, NY)
```

```python
import functools
import jax, jax.numpy as jnp
from jax import lax
from jax.experimental import pallas as pl
from jax.experimental.pallas import tpu as pltpu
from jax.sharding import PartitionSpec as P

NC = 16
ROWS = 32
LANES = 128
ITERS = 4
STEPS = 4
KS = 48
PAIRS = [(i, j) for i in range(NC) for j in range(i, NC)]
PIDX = {p: n for n, p in enumerate(PAIRS)}
NP = len(PAIRS)
M2 = NP + NC


def split2(v):
    hi = v.astype(jnp.bfloat16)
    lo = (v - hi.astype(jnp.float32)).astype(jnp.bfloat16)
    return hi, lo


def speciate_kernel(idx_ref, counts_ref, flags_ref, at3_ref, a3_ref, bias_ref, rate_ref,
                    p0_ref, p1_ref, p2_ref, p3_ref, out_ref,
                    tot_ref, y_ref, jac_ref, l1_ref, l2_ref):
    me = idx_ref[1]
    count = counts_ref[idx_ref[0], me]
    a3 = a3_ref[...]
    hi, lo = split2(a3)
    lane = lax.broadcasted_iota(jnp.int32, a3.shape, 1)
    l1_ref[...] = jnp.where(lane < 2 * NC, hi.astype(jnp.float32), lo.astype(jnp.float32)).astype(jnp.bfloat16)
    at3 = at3_ref[...]
    row = 0
    for i in range(NC + 1):
        tab = at3[i:, :] * at3[i:i + 1, :] if i < NC else at3
        n = tab.shape[0]
        l2_ref[row:row + n, :] = tab
        row += n
    tab = l2_ref[...]
    hi, lo = split2(tab)
    lane = lax.broadcasted_iota(jnp.int32, tab.shape, 1)
    l2 = jnp.where(lane < 2 * KS, hi.astype(jnp.float32), lo.astype(jnp.float32)).astype(jnp.bfloat16)
    l1 = l1_ref[...]
    for k, part in enumerate((p0_ref, p1_ref, p2_ref, p3_ref)):
        base = pl.multiple_of(lax.rem(me - k + 4, 4) * (4 * ROWS), 4 * ROWS)
        val = part[...]
        tot_ref[pl.ds(base, 4 * ROWS), :] = val
        y_ref[pl.ds(base, 4 * ROWS), :] = jnp.log(val)

    def stage(g):
        ys = jnp.concatenate([y_ref[pl.ds(8 * g + r, NC, stride=ROWS), :] for r in range(8)], axis=1)
        y1, y2 = split2(ys)
        s = jnp.dot(l1, jnp.concatenate([y1, y2, y1], axis=0), preferred_element_type=jnp.float32)
        xs = []
        for r in range(8):
            x = jnp.exp(s[:, r * LANES:(r + 1) * LANES] + bias_ref[...])
            m = flags_ref[(8 * g + r) // 2, 0].astype(jnp.float32)
            xs.append(jnp.concatenate([x[:32], x[32:] * (rate_ref[...] * m)], axis=0))
        x1, x2 = split2(jnp.concatenate(xs, axis=1))
        gm = jnp.dot(l2, jnp.concatenate([x1, x2, x1], axis=0), preferred_element_type=jnp.float32)
        for r in range(8):
            jac_ref[pl.ds(8 * g + r, M2, stride=ROWS), :] = gm[:, r * LANES:(r + 1) * LANES]

    def solve(g):
        def jac(p):
            return jac_ref[p * ROWS + 8 * g:p * ROWS + 8 * g + 8, :]
        def cell(ref, k):
            return ref[k * ROWS + 8 * g:k * ROWS + 8 * g + 8, :]
        w = [[None] * NC for _ in range(NC + 1)]
        rd = [None] * NC
        for j in range(NC):
            lj = [w[j][k] * rd[k] for k in range(j)]
            cj = jnp.exp(cell(y_ref, j))
            for i in range(j, NC + 1):
                if i == NC:
                    acc = jac(NP + j) + cj - cell(tot_ref, j)
                else:
                    acc = jac(PIDX[(j, i)])
                    if i == j:
                        acc = acc + cj
                for k in range(j):
                    acc = acc - w[i][k] * lj[k]
                w[i][j] = acc
            rd[j] = 1.0 / w[j][j]
        sol = [None] * NC
        for j in reversed(range(NC)):
            acc = w[NC][j]
            for i in range(j + 1, NC):
                acc = acc - w[i][j] * sol[i]
            sol[j] = acc * rd[j]
        largest = functools.reduce(jnp.maximum, [jnp.abs(v) for v in sol])
        scale = 1.0 / jnp.maximum(largest, 1.0)
        for j in range(NC):
            y_ref[j * ROWS + 8 * g:j * ROWS + 8 * g + 8, :] = cell(y_ref, j) - sol[j] * scale

    stage(0)

    def body(it, carry):
        for g in range(4):
            stage((g + 1) % 4)
            solve(g)
        return carry

    lax.fori_loop(0, ITERS, body, 0)
    for g in range(4):
        front = 8 * g + lax.broadcasted_iota(jnp.int32, (8, LANES), 0) < 2 * count
        for k in range(NC):
            sl = slice(k * ROWS + 8 * g, k * ROWS + 8 * g + 8)
            out_ref[sl, :] = jnp.where(front, y_ref[sl, :], jnp.log(tot_ref[sl, :]))


def tables(stoich, log_k, mineral_stoich, mineral_log_k, mineral_rate):
    nsec, nm = stoich.shape[0], mineral_stoich.shape[0]
    a = jnp.concatenate([stoich, mineral_stoich, jnp.zeros((KS - nsec - nm, NC), jnp.float32)], axis=0)
    a3 = jnp.concatenate([a, a, a], axis=1)
    at = a.T
    at3 = jnp.concatenate([at, at, at], axis=1)
    bias = jnp.concatenate([log_k, -mineral_log_k, jnp.zeros((KS - nsec - nm,), jnp.float32)])
    rate = jnp.concatenate([mineral_rate, jnp.zeros((KS - nsec - nm,), jnp.float32)])
    return at3, a3, jnp.broadcast_to(bias[:, None], (KS, LANES)), jnp.broadcast_to(rate[:, None], (16, LANES))


def speciate(idx, counts, flags, tabs, parts):
    smem = pl.BlockSpec(memory_space=pltpu.SMEM)
    vmem = pl.BlockSpec(memory_space=pltpu.VMEM)
    return pl.pallas_call(
        speciate_kernel,
        out_shape=jax.ShapeDtypeStruct((NC * ROWS, LANES), jnp.float32),
        in_specs=[smem] * 3 + [vmem] * 8,
        out_specs=vmem,
        scratch_shapes=[
            pltpu.VMEM((NC * ROWS, LANES), jnp.float32),
            pltpu.VMEM((NC * ROWS, LANES), jnp.float32),
            pltpu.VMEM((M2 * ROWS, LANES), jnp.float32),
            pltpu.VMEM((KS, 3 * NC), jnp.bfloat16),
            pltpu.VMEM((M2, 3 * KS), jnp.float32),
        ],
        name="speciate",
    )(idx, counts, flags, *tabs, *parts)


HALO = 4


def transport_kernel(idx_ref, before_ref, after_ref, tot_ref, cour_ref, diff_ref,
                     o0_ref, o1_ref, o2_ref, o3_ref, ext_ref, fin_ref):
    width = ext_ref.shape[1]
    zeros = jnp.zeros((4, width), jnp.float32)
    ext_ref[0:4, :] = zeros
    ext_ref[44:48, :] = zeros

    def extend(own, part):
        ext_ref[4:8, :] = before_ref[part]
        ext_ref[8:40, :] = own
        ext_ref[40:44, :] = after_ref[part]
        return ext_ref[...]

    courant = extend(cour_ref[...], 4)
    diffusion = extend(diff_ref[...], 5)
    keep = 1.0 - courant - 4.0 * diffusion
    behind = courant + diffusion
    col = lax.broadcasted_iota(jnp.int32, (48, width), 1)
    for c in range(4):
        f = extend(tot_ref[c], c)
        for step in range(STEPS):
            up = pltpu.roll(f, 1, 0)
            down = pltpu.roll(f, 47, 0)
            left = jnp.where(col == 0, 0.0, pltpu.roll(f, 1, 1))
            right = jnp.where(col == width - 1, 0.0, pltpu.roll(f, width - 1, 1))
            f = keep * f + behind * up + diffusion * (down + (left + right))
        fin_ref[c * ROWS:(c + 1) * ROWS, :] = f[8:40, :]
    me = idx_ref[1]
    for k, out_ref in enumerate((o0_ref, o1_ref, o2_ref, o3_ref)):
        start = pl.multiple_of(lax.rem(me + k, 4) * LANES, LANES)
        out_ref[...] = fin_ref[:, pl.ds(start, LANES)]


def transport(idx, before, after, totals, courant, diffusion):
    smem = pl.BlockSpec(memory_space=pltpu.SMEM)
    vmem = pl.BlockSpec(memory_space=pltpu.VMEM)
    width = totals.shape[2]
    return pl.pallas_call(
        transport_kernel,
        out_shape=[jax.ShapeDtypeStruct((4 * ROWS, LANES), jnp.float32)] * 4,
        in_specs=[smem] + [vmem] * 5,
        out_specs=[vmem] * 4,
        scratch_shapes=[
            pltpu.VMEM((48, width), jnp.float32),
            pltpu.VMEM((4 * ROWS, width), jnp.float32),
        ],
        name="transport",
    )(idx, before, after, totals, courant, diffusion)


def shards(totals, courant, diffusion, stoich, log_k, mineral_stoich, mineral_log_k,
           mineral_rate, front_counts, mineral_flags):
    idx = jnp.stack([lax.axis_index("wide"), lax.axis_index("narrow")]).astype(jnp.int32)
    count = lax.axis_size("wide")
    up = [(i, i + 1) for i in range(count - 1)]
    down = [(i + 1, i) for i in range(count - 1)]

    def rows(start, stop):
        return jnp.concatenate(
            [totals[:, start:stop], courant[None, start:stop], diffusion[None, start:stop]], axis=0)

    before = lax.ppermute(rows(ROWS - HALO, ROWS), "wide", up)
    after = lax.ppermute(rows(0, HALO), "wide", down)
    own = transport(idx, before, after, totals, courant, diffusion)
    parts = [own[0]]
    for k in (1, 2, 3):
        parts.append(lax.ppermute(own[k], "narrow", [(i, (i + k) % 4) for i in range(4)]))
    tabs = tables(stoich, log_k, mineral_stoich, mineral_log_k, mineral_rate)
    out = speciate(idx, front_counts, mineral_flags, tabs, parts)
    return out.reshape(NC, ROWS, LANES)


def solution(mesh):
    placed = (
        P("narrow", "wide", None), P("wide", None), P("wide", None),
        P(), P(), P(), P(), P(), P(), P("wide", "narrow"),
    )
    return jax.shard_map(
        shards, mesh=mesh, in_specs=placed, out_specs=P(None, "wide", "narrow"), check_vma=False
    )
```

```python
import functools

import jax
import jax.numpy as jnp
from jax import lax
from jax.experimental import pallas as pl
from jax.experimental.pallas import tpu as pltpu
from jax.sharding import PartitionSpec as P

STEPS = 4
ITERS = 4
HALO = 4
CHUNK = 8
NC = 16
ROWS = 32
LANES = 128
NBLK = 16
NSEC = 32
NM = 12
KS = 48
OFF = -16384.0
PITCH = 33
LOG2E = 1.4426950408889634
LN2 = 0.6931471805599453
PAIRS = [(i, j) for i in range(NC) for j in range(i, NC)]
PIDX = {p: n for n, p in enumerate(PAIRS)}
NP = len(PAIRS)
M2 = NP + NC
HBM = pl.BlockSpec(memory_space=pl.ANY)
VMEM = pl.BlockSpec(memory_space=pltpu.VMEM)


def on_chip(x):
    return pltpu.with_memory_space_constraint(x, pltpu.VMEM)


def in_hbm(x):
    return pltpu.with_memory_space_constraint(x, pltpu.HBM)


def vmem_out(shape, dtype=jnp.float32):
    return pltpu.VMEM(shape, dtype)


def split2(v):
    hi = v.astype(jnp.bfloat16)
    lo = (v - hi.astype(jnp.float32)).astype(jnp.bfloat16)
    return hi, lo


def is_even():
    return lax.rem(lax.axis_index("wide"), 2) == 0


def pack_kernel(tot_ref, cour_ref, diff_ref, pair_ref, next_ref, edge_ref, sems):
    copies = []
    for side, start in enumerate((0, ROWS - 8)):
        for n, (src, dst) in enumerate((
            (tot_ref.at[:, start:start + 8, :], edge_ref.at[side, 0:4]),
            (cour_ref.at[start:start + 8, :], edge_ref.at[side, 4]),
            (diff_ref.at[start:start + 8, :], edge_ref.at[side, 5]),
        )):
            copies.append(pltpu.make_async_copy(src, dst, sems.at[3 * side + n]))
    for c in copies:
        c.start()
    for c in copies:
        c.wait()
    first = edge_ref[0, :, 0:HALO, :]
    last = edge_ref[1, :, 8 - HALO:8, :]
    even = is_even()
    pair_ref[...] = jnp.where(even, last, first)
    next_ref[...] = jnp.where(even, first, last)


def pack(totals, courant, diffusion):
    width = totals.shape[2]
    return pl.pallas_call(
        pack_kernel,
        out_shape=[vmem_out((6, HALO, width))] * 2,
        in_specs=[HBM] * 3,
        out_specs=[VMEM] * 2,
        scratch_shapes=[pltpu.VMEM((2, 6, 8, width), jnp.float32), pltpu.SemaphoreType.DMA((6,))],
        compiler_params=pltpu.CompilerParams(vmem_limit_bytes=4 << 20),
        name="pack",
    )(*[in_hbm(v) for v in (totals, courant, diffusion)])


def transport_kernel(pair_ref, next_ref, tot_ref, cour_ref, diff_ref, out_ref, buf_ref, coef_ref, res_ref, sems):
    tiles = buf_ref.shape[2]
    even = is_even()
    parts = [slice(k * LANES, (k + 1) * LANES) for k in range(tiles)]
    zeros = jnp.zeros((8, LANES), jnp.float32)
    for slot in range(2):
        for c in range(4):
            for k in range(tiles):
                buf_ref[slot, c, k, 0:8, :] = zeros
                buf_ref[slot, c, k, 48:56, :] = zeros

    def extend(dst, own, part):
        before = jnp.where(even, next_ref[part], pair_ref[part])
        after = jnp.where(even, pair_ref[part], next_ref[part])
        for k, cols in enumerate(parts):
            dst[k, 8:12, :] = before[:, cols]
            dst[k, 12:44, :] = own[:, cols]
            dst[k, 44:48, :] = after[:, cols]

    extend(coef_ref.at[0], cour_ref[...], 4)
    extend(coef_ref.at[1], diff_ref[...], 5)
    mid = slice(8, 48)
    for k in range(tiles):
        u, d = coef_ref[0, k, mid, :], coef_ref[1, k, mid, :]
        coef_ref[2, k, mid, :] = 1.0 - u - 4.0 * d
        coef_ref[0, k, mid, :] = u + d
    for c in range(4):
        extend(buf_ref.at[0, c], tot_ref[c], c)
    lane = lax.broadcasted_iota(jnp.int32, (40, LANES), 1)
    copies = []
    for step in range(STEPS):
        src, dst = step % 2, (step + 1) % 2
        for c in range(4):
            f = [buf_ref[src, c, k, mid, :] for k in range(tiles)]
            right = [pltpu.roll(v, 1, 1) for v in f]
            left = [pltpu.roll(v, LANES - 1, 1) for v in f]
            for k in range(tiles):
                west = jnp.where(lane == 0, right[k - 1] if k else 0.0, right[k])
                east = jnp.where(lane == LANES - 1, left[k + 1] if k + 1 < tiles else 0.0, left[k])
                up = buf_ref[src, c, k, 7:47, :]
                down = buf_ref[src, c, k, 9:49, :]
                new = coef_ref[2, k, mid, :] * f[k] + coef_ref[0, k, mid, :] * up
                new = new + coef_ref[1, k, mid, :] * (down + (west + east))
                buf_ref[dst, c, k, mid, :] = new
            if step == STEPS - 1:
                rows = slice(c * ROWS, (c + 1) * ROWS)
                for k in range(tiles):
                    res_ref[k, rows, :] = buf_ref[dst, c, k, 12:44, :]
                copies.append(pltpu.make_async_copy(res_ref.at[:, rows, :], out_ref.at[:, rows, :], sems.at[c]))
                copies[-1].start()
    for c in copies:
        c.wait()


def transport(pair, nxt, totals, courant, diffusion):
    tiles = totals.shape[2] // LANES
    return pl.pallas_call(
        transport_kernel,
        out_shape=jax.ShapeDtypeStruct((4, 4 * ROWS, LANES), jnp.float32),
        in_specs=[VMEM] * 5,
        out_specs=HBM,
        scratch_shapes=[
            pltpu.VMEM((2, 4, tiles, 56, LANES), jnp.float32),
            pltpu.VMEM((3, tiles, 56, LANES), jnp.float32),
            pltpu.VMEM((4, 4 * ROWS, LANES), jnp.float32),
            pltpu.SemaphoreType.DMA((4,)),
        ],
        compiler_params=pltpu.CompilerParams(vmem_limit_bytes=8 << 20),
        name="transport",
    )(*[on_chip(v) for v in (pair, nxt, totals, courant, diffusion)])


def tables_kernel(st_ref, ms_ref, lk_ref, mk_ref, mr_ref, counts_ref, flags_ref,
                  l1_ref, l2_ref, unit_ref, front_ref,
                  sq_ref, tab_ref, vec_ref, st, ms, lks, mks, mrs, cs, fs, sems):
    wide, narrow = lax.axis_index("wide"), lax.axis_index("narrow")
    copies = [pltpu.make_async_copy(src, dst, sems.at[n]) for n, (src, dst) in enumerate((
        (st_ref, st), (ms_ref, ms), (lk_ref, lks), (mk_ref, mks), (mr_ref, mrs), (counts_ref, cs), (flags_ref, fs)))]
    for c in copies:
        c.start()
    sq_ref[...] = jnp.zeros(sq_ref.shape, jnp.float32)
    vec_ref[...] = jnp.zeros(vec_ref.shape, jnp.float32)
    vec_ref[2:3, :] = jnp.ones((1, LANES), jnp.float32)
    for c in copies:
        c.wait()
    sq_ref[0, 0:NC, 0:NSEC] = st[...]
    sq_ref[1, NSEC:NSEC + NM, 0:NC] = ms[...]
    vec_ref[0:1, 0:NSEC] = lks[...]
    vec_ref[1:2, 0:NM] = mks[...]
    vec_ref[2:3, 0:NM] = mrs[...]
    at = sq_ref[0] + sq_ref[1].T
    vec = vec_ref[...]
    shifted = pltpu.roll(vec * -LOG2E, NSEC, 1)[1:2, :] + pltpu.roll(jnp.log(vec_ref[2:3, :]) * LOG2E, NSEC, 1)
    bias = vec[0:1, :] * LOG2E + shifted
    lane = lax.broadcasted_iota(jnp.int32, (1, LANES), 1)
    off = jnp.where((lane >= NSEC) & (lane < NSEC + NM), OFF, 0.0)
    hi, lo = split2(at[0:NC, :])
    b1, b2 = split2(bias)
    b3 = (bias - b1.astype(jnp.float32)) - b2.astype(jnp.float32)
    sq_ref[0, 0:NC, :] = hi.astype(jnp.float32)
    sq_ref[0, NC:2 * NC, :] = hi.astype(jnp.float32)
    sq_ref[0, 2 * NC:3 * NC, :] = lo.astype(jnp.float32)
    sq_ref[0, 48:49, :] = b1.astype(jnp.float32)
    sq_ref[0, 49:50, :] = b2.astype(jnp.float32)
    sq_ref[0, 50:51, :] = b3
    sq_ref[0, 51:52, :] = off
    l1_ref[...] = sq_ref[0].T[0:KS, 0:4 * NC].astype(jnp.bfloat16)
    row = 0
    for i in range(NC + 1):
        tab = at[i:NC, :] * at[i:i + 1, :] if i < NC else at[0:NC, :]
        n = tab.shape[0]
        tab_ref[row:row + n, :] = tab
        row += n
    hi, lo = split2(tab_ref[...])
    hi, lo = hi.astype(jnp.float32), lo.astype(jnp.float32)
    lo = pltpu.roll(lo, 2 * KS, 1)
    lane = lax.broadcasted_iota(jnp.int32, lo.shape, 1)
    l2_ref[:, 0:128] = jnp.where(lane < 2 * KS, hi + pltpu.roll(hi, KS, 1), lo).astype(jnp.bfloat16)
    l2_ref[:, 128:3 * KS] = lo[:, 0:3 * KS - 128].astype(jnp.bfloat16)
    row = lax.broadcasted_iota(jnp.int32, (16, LANES), 0)
    for b in range(NBLK):
        absent = 1.0 - fs[b].astype(jnp.float32)
        unit_ref[b] = jnp.where(row < 3, 1.0, jnp.where(row == 3, absent, 0.0)).astype(jnp.bfloat16)
    count = cs[narrow, wide]
    front_ref[...] = jnp.where(lax.broadcasted_iota(jnp.int32, (ROWS, LANES), 0) < 2 * count, 1.0, 0.0)


def tables(stoich, mineral_stoich, log_k, mineral_log_k, mineral_rate, counts, flags):
    return pl.pallas_call(
        tables_kernel,
        out_shape=[vmem_out((KS, 4 * NC), jnp.bfloat16), vmem_out((M2, 3 * KS), jnp.bfloat16),
                   vmem_out((NBLK, 16, LANES), jnp.bfloat16), vmem_out((ROWS, LANES))],
        in_specs=[HBM] * 7,
        out_specs=[VMEM] * 4,
        scratch_shapes=[
            pltpu.VMEM((2, 128, 128), jnp.float32), pltpu.VMEM((M2, 128), jnp.float32), pltpu.VMEM((8, LANES), jnp.float32),
            pltpu.VMEM((NC, NSEC), jnp.float32), pltpu.VMEM((NM, NC), jnp.float32),
            pltpu.VMEM((1, NSEC), jnp.float32), pltpu.VMEM((1, NM), jnp.float32), pltpu.VMEM((1, NM), jnp.float32),
            pltpu.SMEM(counts.shape, jnp.int32), pltpu.SMEM((NBLK,), jnp.int32),
            pltpu.SemaphoreType.DMA((7,)),
        ],
        compiler_params=pltpu.CompilerParams(vmem_limit_bytes=4 << 20),
        name="tables",
    )(*[in_hbm(v) for v in (stoich, mineral_stoich, log_k, mineral_log_k, mineral_rate, counts, flags)])


def speciate_kernel(l1_ref, l2_ref, unit_ref, front_ref, tot_ref, out_ref, y_ref, jac_ref, res_ref, sems):
    for k in range(NC):
        start = jnp.log(tot_ref[k * ROWS:(k + 1) * ROWS, :])
        res_ref[k] = start
        y_ref[k * PITCH:k * PITCH + ROWS, :] = start * LOG2E
    l1 = l1_ref[...]
    l2 = l2_ref[...]

    def stage(g):
        rows = range(8 * g, 8 * g + 8)
        ys = jnp.concatenate([y_ref[pl.ds(r, NC, stride=PITCH), :] for r in rows], axis=1)
        unit = jnp.concatenate([unit_ref[r // 2] for r in rows], axis=1)
        y1, y2 = split2(ys)
        s = jnp.dot(l1, jnp.concatenate([y1, y2, y1, unit], axis=0), preferred_element_type=jnp.float32)
        x1, x2 = split2(jnp.exp2(s))
        gm = jnp.dot(l2, jnp.concatenate([x1, x2, x1], axis=0), preferred_element_type=jnp.float32)
        for n, r in enumerate(rows):
            jac_ref[pl.ds(r, M2, stride=PITCH), :] = gm[:, n * LANES:(n + 1) * LANES]

    def solve(groups):
        def jac(p, g):
            return jac_ref[p * PITCH + 8 * g:p * PITCH + 8 * g + 8, :]

        def ysl(k, g):
            return slice(k * PITCH + 8 * g, k * PITCH + 8 * g + 8)

        w = {g: [[None] * NC for _ in range(NC + 1)] for g in groups}
        rd = {g: [None] * NC for g in groups}
        for j in range(NC):
            lj = {g: [w[g][j][k] * rd[g][k] for k in range(j)] for g in groups}
            for i in range(j, NC + 1):
                for g in groups:
                    if i == NC:
                        acc = jac(NP + j, g) + jnp.exp2(y_ref[ysl(j, g), :]) - tot_ref[j * ROWS + 8 * g:j * ROWS + 8 * g + 8, :]
                    else:
                        acc = jac(PIDX[(j, i)], g)
                        if i == j:
                            acc = acc + jnp.exp2(y_ref[ysl(j, g), :])
                    for k in range(j):
                        acc = acc - w[g][i][k] * lj[g][k]
                    w[g][i][j] = acc
                    if i == j:
                        rd[g][j] = 1.0 / acc
        sol = {g: [None] * NC for g in groups}
        for j in reversed(range(NC)):
            for g in groups:
                acc = w[g][NC][j]
                for i in reversed(range(j + 1, NC)):
                    acc = acc - w[g][i][j] * sol[g][i]
                sol[g][j] = acc * rd[g][j]
        for g in groups:
            largest = functools.reduce(jnp.maximum, [jnp.abs(v) for v in sol[g]])
            scale = LOG2E / jnp.maximum(largest, 1.0)
            for j in range(NC):
                y_ref[ysl(j, g), :] = y_ref[ysl(j, g), :] - sol[g][j] * scale

    copies = []

    def finish(half):
        rows = slice(16 * half, 16 * half + 16)
        front = front_ref[rows, :] > 0.5
        for k in range(NC):
            sol = y_ref[k * PITCH + 16 * half:k * PITCH + 16 * half + 16, :] * LN2
            res_ref[k, rows, :] = jnp.where(front, sol, res_ref[k, rows, :])
        copies.append(pltpu.make_async_copy(res_ref.at[:, rows, :], out_ref.at[:, rows, :], sems.at[half]))
        copies[-1].start()

    stage(0)
    stage(1)
    for it in range(ITERS):
        stage(2)
        stage(3)
        solve((0, 1))
        if it < ITERS - 1:
            stage(0)
            stage(1)
        else:
            finish(0)
        solve((2, 3))
    finish(1)
    for c in copies:
        c.wait()


def speciate(tabs, total):
    return pl.pallas_call(
        speciate_kernel,
        out_shape=jax.ShapeDtypeStruct((NC, ROWS, LANES), jnp.float32),
        in_specs=[VMEM] * 5,
        out_specs=HBM,
        scratch_shapes=[
            pltpu.VMEM((NC * PITCH, LANES), jnp.float32),
            pltpu.VMEM((M2 * PITCH, LANES), jnp.float32),
            pltpu.VMEM((NC, ROWS, LANES), jnp.float32),
            pltpu.SemaphoreType.DMA((2,)),
        ],
        compiler_params=pltpu.CompilerParams(vmem_limit_bytes=16 << 20),
        name="speciate",
    )(*[on_chip(v) for v in tabs], on_chip(total))


def shards(totals, courant, diffusion, stoich, log_k, mineral_stoich, mineral_log_k,
           mineral_rate, front_counts, mineral_flags):
    count = lax.axis_size("wide")
    pairs = [(i, i ^ 1) for i in range(count)]
    across = [(i, ((i + 1) ^ 1) - 1) for i in range(1, count - 1)]
    to_pair, to_next = pack(totals, courant, diffusion)
    pair = lax.ppermute(to_pair, "wide", pairs)
    nxt = lax.ppermute(to_next, "wide", across)
    moved = transport(pair, nxt, totals, courant, diffusion)
    total = lax.all_to_all(moved, "narrow", split_axis=0, concat_axis=0)
    tabs = tables(stoich.T, mineral_stoich, log_k.reshape(1, NSEC), mineral_log_k.reshape(1, NM), mineral_rate.reshape(1, NM),
                  front_counts.T, mineral_flags.reshape(NBLK))
    return speciate(tabs, total.reshape(NC * ROWS, LANES))


def solution(mesh):
    placed = (
        P("narrow", "wide", None), P("wide", None), P("wide", None),
        P(), P(), P(), P(), P(), P(), P("wide", "narrow"),
    )
    return jax.shard_map(
        shards, mesh=mesh, in_specs=placed, out_specs=P(None, "wide", "narrow"), check_vma=False
    )
```

```python
import functools

import jax
import jax.numpy as jnp
from jax import lax
from jax.experimental import pallas as pl
from jax.experimental.pallas import tpu as pltpu
from jax.sharding import PartitionSpec as P


STEPS = 4
ITERS = 4
HALO = 4
EARLY, LATE = 4, 2
NC = 16
ROWS = 32
LANES = 128
NBLK = 16
NSEC = 32
NM = 12
KS = 48
OFF = -16384.0
PITCH = 33
LOG2E = 1.4426950408889634
LN2 = 0.6931471805599453
PAIRS = [(i, j) for i in range(NC) for j in range(i, NC)]
PIDX = {p: n for n, p in enumerate(PAIRS)}
NP = len(PAIRS)
M2 = NP + NC
HBM = pl.BlockSpec(memory_space=pl.ANY)
VMEM = pl.BlockSpec(memory_space=pltpu.VMEM)


def on_chip(x):
    return pltpu.with_memory_space_constraint(x, pltpu.VMEM)


def in_hbm(x):
    return pltpu.with_memory_space_constraint(x, pltpu.HBM)


def vmem_out(shape, dtype=jnp.float32):
    return pltpu.VMEM(shape, dtype)


def split2(v):
    hi = v.astype(jnp.bfloat16)
    lo = (v - hi.astype(jnp.float32)).astype(jnp.bfloat16)
    return hi, lo


def is_even():
    return lax.rem(lax.axis_index("wide"), 2) == 0


def pack_kernel(tot_ref, cour_ref, diff_ref, pair_ref, next_ref, edge_ref, sems):
    copies = []
    for side, start in enumerate((0, ROWS - 8)):
        for n, (src, dst) in enumerate((
            (tot_ref.at[:, start:start + 8, :], edge_ref.at[side, 0:4]),
            (cour_ref.at[start:start + 8, :], edge_ref.at[side, 4]),
            (diff_ref.at[start:start + 8, :], edge_ref.at[side, 5]),
        )):
            copies.append(pltpu.make_async_copy(src, dst, sems.at[3 * side + n]))
    for c in copies:
        c.start()
    for c in copies:
        c.wait()
    first = edge_ref[0, :, 0:HALO, :]
    last = edge_ref[1, :, 8 - HALO:8, :]
    even = is_even()
    pair_ref[...] = jnp.where(even, last, first)
    next_ref[...] = jnp.where(even, first, last)


def pack(totals, courant, diffusion):
    width = totals.shape[2]
    return pl.pallas_call(
        pack_kernel,
        out_shape=[vmem_out((6, HALO, width))] * 2,
        in_specs=[HBM] * 3,
        out_specs=[VMEM] * 2,
        scratch_shapes=[pltpu.VMEM((2, 6, 8, width), jnp.float32), pltpu.SemaphoreType.DMA((6,))],
        compiler_params=pltpu.CompilerParams(vmem_limit_bytes=4 << 20),
        name="pack",
    )(*[in_hbm(v) for v in (totals, courant, diffusion)])


def transport_kernel(pair_ref, next_ref, tot_ref, cour_ref, diff_ref, out_ref, buf_ref, coef_ref, res_ref, sems):
    tiles = buf_ref.shape[2]
    even = is_even()
    parts = [slice(k * LANES, (k + 1) * LANES) for k in range(tiles)]
    zeros = jnp.zeros((8, LANES), jnp.float32)
    for slot in range(2):
        for c in range(4):
            for k in range(tiles):
                buf_ref[slot, c, k, 0:8, :] = zeros
                buf_ref[slot, c, k, 48:56, :] = zeros

    def extend(dst, own, part):
        before = jnp.where(even, next_ref[part], pair_ref[part])
        after = jnp.where(even, pair_ref[part], next_ref[part])
        for k, cols in enumerate(parts):
            dst[k, 8:12, :] = before[:, cols]
            dst[k, 12:44, :] = own[:, cols]
            dst[k, 44:48, :] = after[:, cols]

    extend(coef_ref.at[0], cour_ref[...], 4)
    extend(coef_ref.at[1], diff_ref[...], 5)
    mid = slice(8, 48)
    for k in range(tiles):
        u, d = coef_ref[0, k, mid, :], coef_ref[1, k, mid, :]
        coef_ref[2, k, mid, :] = 1.0 - u - 4.0 * d
        coef_ref[0, k, mid, :] = u + d
    for c in range(4):
        extend(buf_ref.at[0, c], tot_ref[c], c)
    copies = []

    def advance(step, c):
        src, dst = step % 2, (step + 1) % 2
        last = step == STEPS - 1
        lo, hi = (12, 44) if last else (8, 48)
        rows = slice(lo, hi)
        lane = lax.broadcasted_iota(jnp.int32, (hi - lo, LANES), 1)
        f = [buf_ref[src, c, k, rows, :] for k in range(tiles)]
        right = [pltpu.roll(v, 1, 1) for v in f]
        left = [pltpu.roll(v, LANES - 1, 1) for v in f]
        for k in range(tiles):
            west = jnp.where(lane == 0, right[k - 1] if k else 0.0, right[k])
            east = jnp.where(lane == LANES - 1, left[k + 1] if k + 1 < tiles else 0.0, left[k])
            up = buf_ref[src, c, k, lo - 1:hi - 1, :]
            down = buf_ref[src, c, k, lo + 1:hi + 1, :]
            new = coef_ref[2, k, rows, :] * f[k] + coef_ref[0, k, rows, :] * up
            new = new + coef_ref[1, k, rows, :] * (down + (west + east))
            if last:
                res_ref[k, c * ROWS:(c + 1) * ROWS, :] = new
            else:
                buf_ref[dst, c, k, rows, :] = new
        if last:
            own = slice(c * ROWS, (c + 1) * ROWS)
            copies.append(pltpu.make_async_copy(res_ref.at[:, own, :], out_ref.at[:, own, :], sems.at[c]))
            copies[-1].start()

    for step in range(STEPS):
        for c in range(4):
            advance(step, c)
    for c in copies:
        c.wait()


def transport(pair, nxt, totals, courant, diffusion):
    tiles = totals.shape[2] // LANES
    return pl.pallas_call(
        transport_kernel,
        out_shape=jax.ShapeDtypeStruct((4, 4 * ROWS, LANES), jnp.float32),
        in_specs=[VMEM] * 5,
        out_specs=HBM,
        scratch_shapes=[
            pltpu.VMEM((2, 4, tiles, 56, LANES), jnp.float32),
            pltpu.VMEM((3, tiles, 56, LANES), jnp.float32),
            pltpu.VMEM((4, 4 * ROWS, LANES), jnp.float32),
            pltpu.SemaphoreType.DMA((4,)),
        ],
        compiler_params=pltpu.CompilerParams(vmem_limit_bytes=8 << 20),
        name="transport",
    )(*[on_chip(v) for v in (pair, nxt, totals, courant, diffusion)])


def tables_kernel(st_ref, ms_ref, lk_ref, mk_ref, mr_ref, counts_ref, flags_ref,
                  l1_ref, l2_ref, unit_ref, front_ref,
                  sq_ref, tab_ref, vec_ref, st, ms, lks, mks, mrs, cs, fs, sems):
    wide, narrow = lax.axis_index("wide"), lax.axis_index("narrow")
    copies = [pltpu.make_async_copy(src, dst, sems.at[n]) for n, (src, dst) in enumerate((
        (st_ref, st), (ms_ref, ms), (lk_ref, lks), (mk_ref, mks), (mr_ref, mrs), (counts_ref, cs), (flags_ref, fs)))]
    for c in copies:
        c.start()
    sq_ref[...] = jnp.zeros(sq_ref.shape, jnp.float32)
    vec_ref[...] = jnp.zeros(vec_ref.shape, jnp.float32)
    vec_ref[2:3, :] = jnp.ones((1, LANES), jnp.float32)
    for c in copies:
        c.wait()
    sq_ref[0, 0:NC, 0:NSEC] = st[...]
    sq_ref[1, NSEC:NSEC + NM, 0:NC] = ms[...]
    vec_ref[0:1, 0:NSEC] = lks[...]
    vec_ref[1:2, 0:NM] = mks[...]
    vec_ref[2:3, 0:NM] = mrs[...]
    at = sq_ref[0] + sq_ref[1].T
    vec = vec_ref[...]
    shifted = pltpu.roll(vec * -LOG2E, NSEC, 1)[1:2, :] + pltpu.roll(jnp.log(vec_ref[2:3, :]) * LOG2E, NSEC, 1)
    bias = vec[0:1, :] * LOG2E + shifted
    lane = lax.broadcasted_iota(jnp.int32, (1, LANES), 1)
    off = jnp.where((lane >= NSEC) & (lane < NSEC + NM), OFF, 0.0)
    hi, lo = split2(at[0:NC, :])
    b1, b2 = split2(bias)
    b3 = (bias - b1.astype(jnp.float32)) - b2.astype(jnp.float32)
    sq_ref[0, 0:NC, :] = hi.astype(jnp.float32)
    sq_ref[0, NC:2 * NC, :] = hi.astype(jnp.float32)
    sq_ref[0, 2 * NC:3 * NC, :] = lo.astype(jnp.float32)
    sq_ref[0, 48:49, :] = b1.astype(jnp.float32)
    sq_ref[0, 49:50, :] = b2.astype(jnp.float32)
    sq_ref[0, 50:51, :] = b3
    sq_ref[0, 51:52, :] = off
    l1_ref[...] = sq_ref[0].T[0:KS, 0:4 * NC].astype(jnp.bfloat16)
    row = 0
    for i in range(NC + 1):
        tab = at[i:NC, :] * at[i:i + 1, :] if i < NC else at[0:NC, :]
        n = tab.shape[0]
        tab_ref[row:row + n, :] = tab
        row += n
    hi, lo = split2(tab_ref[...])
    hi, lo = hi.astype(jnp.float32), lo.astype(jnp.float32)
    lo = pltpu.roll(lo, 2 * KS, 1)
    lane = lax.broadcasted_iota(jnp.int32, lo.shape, 1)
    l2_ref[:, 0:128] = jnp.where(lane < 2 * KS, hi + pltpu.roll(hi, KS, 1), lo).astype(jnp.bfloat16)
    l2_ref[:, 128:3 * KS] = lo[:, 0:3 * KS - 128].astype(jnp.bfloat16)
    row = lax.broadcasted_iota(jnp.int32, (16, LANES), 0)
    for b in range(NBLK):
        absent = 1.0 - fs[b].astype(jnp.float32)
        unit_ref[b] = jnp.where(row < 3, 1.0, jnp.where(row == 3, absent, 0.0)).astype(jnp.bfloat16)
    count = cs[narrow, wide]
    front_ref[...] = jnp.where(lax.broadcasted_iota(jnp.int32, (ROWS, LANES), 0) < 2 * count, 1.0, 0.0)


def tables(stoich, mineral_stoich, log_k, mineral_log_k, mineral_rate, counts, flags):
    return pl.pallas_call(
        tables_kernel,
        out_shape=[vmem_out((KS, 4 * NC), jnp.bfloat16), vmem_out((M2, 3 * KS), jnp.bfloat16),
                   vmem_out((NBLK, 16, LANES), jnp.bfloat16), vmem_out((ROWS, LANES))],
        in_specs=[HBM] * 7,
        out_specs=[VMEM] * 4,
        scratch_shapes=[
            pltpu.VMEM((2, 128, 128), jnp.float32), pltpu.VMEM((M2, 128), jnp.float32), pltpu.VMEM((8, LANES), jnp.float32),
            pltpu.VMEM((NC, NSEC), jnp.float32), pltpu.VMEM((NM, NC), jnp.float32),
            pltpu.VMEM((1, NSEC), jnp.float32), pltpu.VMEM((1, NM), jnp.float32), pltpu.VMEM((1, NM), jnp.float32),
            pltpu.SMEM(counts.shape, jnp.int32), pltpu.SMEM((NBLK,), jnp.int32),
            pltpu.SemaphoreType.DMA((7,)),
        ],
        compiler_params=pltpu.CompilerParams(vmem_limit_bytes=4 << 20),
        name="tables",
    )(*[in_hbm(v) for v in (stoich, mineral_stoich, log_k, mineral_log_k, mineral_rate, counts, flags)])


def speciate_kernel(l1_ref, l2_ref, unit_ref, front_ref, tot_ref, out_ref, y_ref, jac_ref, res_ref, sems):
    for k in range(NC):
        start = jnp.log(tot_ref[k * ROWS:(k + 1) * ROWS, :])
        res_ref[k] = start
        y_ref[k * PITCH:k * PITCH + ROWS, :] = start * LOG2E
    l1 = l1_ref[...]
    l2 = l2_ref[...]

    def stage(groups):
        s, x = {}, {}
        for g in groups:
            rows = range(8 * g, 8 * g + 8)
            ys = jnp.concatenate([y_ref[pl.ds(r, NC, stride=PITCH), :] for r in rows], axis=1)
            unit = jnp.concatenate([unit_ref[r // 2] for r in rows], axis=1)
            y1, y2 = split2(ys)
            s[g] = jnp.dot(l1, jnp.concatenate([y1, y2, y1, unit], axis=0), preferred_element_type=jnp.float32)
            yield
        for g in groups:
            x1, x2 = split2(jnp.exp2(s[g]))
            x[g] = jnp.concatenate([x1, x2, x1], axis=0)
            yield
            gm = jnp.dot(l2, x[g], preferred_element_type=jnp.float32)
            for n in range(8):
                jac_ref[pl.ds(8 * g + n, M2, stride=PITCH), :] = gm[:, n * LANES:(n + 1) * LANES]
            yield

    def solve(groups):
        def jac(p, g):
            return jac_ref[p * PITCH + 8 * g:p * PITCH + 8 * g + 8, :]

        def ysl(k, g):
            return slice(k * PITCH + 8 * g, k * PITCH + 8 * g + 8)

        w = {g: [[None] * NC for _ in range(NC + 1)] for g in groups}
        rd = {g: [None] * NC for g in groups}
        for j in range(NC):
            lj = {g: [w[g][j][k] * rd[g][k] for k in range(j)] for g in groups}
            for i in range(j, NC + 1):
                for g in groups:
                    if i == NC:
                        acc = jac(NP + j, g) + jnp.exp2(y_ref[ysl(j, g), :]) - tot_ref[j * ROWS + 8 * g:j * ROWS + 8 * g + 8, :]
                    else:
                        acc = jac(PIDX[(j, i)], g)
                        if i == j:
                            acc = acc + jnp.exp2(y_ref[ysl(j, g), :])
                    for k in range(j):
                        acc = acc - w[g][i][k] * lj[g][k]
                    w[g][i][j] = acc
                    if i == j:
                        rd[g][j] = 1.0 / acc
            yield
        sol = {g: [None] * NC for g in groups}
        for j in reversed(range(NC)):
            for g in groups:
                acc = w[g][NC][j]
                for i in reversed(range(j + 1, NC)):
                    acc = acc - w[g][i][j] * sol[g][i]
                sol[g][j] = acc * rd[g][j]
            yield
        for g in groups:
            largest = functools.reduce(jnp.maximum, [jnp.abs(v) for v in sol[g]])
            scale = LOG2E / jnp.maximum(largest, 1.0)
            for j in range(NC):
                y_ref[ysl(j, g), :] = y_ref[ysl(j, g), :] - sol[g][j] * scale
        yield

    def out_copy(half):
        rows = slice(16 * half, 16 * half + 16)
        return pltpu.make_async_copy(res_ref.at[:, rows, :], out_ref.at[:, rows, :], sems.at[half])

    def finish(half):
        rows = slice(16 * half, 16 * half + 16)
        front = front_ref[rows, :] > 0.5
        for k in range(NC):
            sol = y_ref[k * PITCH + 16 * half:k * PITCH + 16 * half + 16, :] * LN2
            res_ref[k, rows, :] = jnp.where(front, sol, res_ref[k, rows, :])
        out_copy(half).start()

    def weave(*plans):
        slots = sorted((step / count, n) for n, (_, count) in enumerate(plans) for step in range(count))
        for _, n in slots:
            next(plans[n][0])

    halves = ((0, 1), (2, 3))
    pieces = 6
    both = front_ref[16, 0] > 0.5

    @pl.when(both)
    def _():
        weave((stage(halves[0]), pieces))
        now = solve(halves[0])
        weave((now, EARLY))
        for turn in range(2 * ITERS):
            half = turn % 2
            other = None
            if turn + 1 < 2 * ITERS:
                weave((now, NC - EARLY - LATE), (stage(halves[1 - half]), pieces))
                other = solve(halves[1 - half])
                weave((now, LATE + NC + 1), (other, EARLY))
            else:
                weave((now, NC - EARLY + NC + 1))
            if turn >= 2 * ITERS - 2:
                finish(half)
            now = other

    @pl.when(jnp.logical_not(both))
    def _():
        out_copy(1).start()

        def body(it, carry):
            weave((stage(halves[0]), pieces))
            weave((solve(halves[0]), 2 * NC + 1))
            return carry

        lax.fori_loop(0, ITERS, body, 0)
        finish(0)

    out_copy(0).wait()
    out_copy(1).wait()


def speciate(tabs, total):
    return pl.pallas_call(
        speciate_kernel,
        out_shape=jax.ShapeDtypeStruct((NC, ROWS, LANES), jnp.float32),
        in_specs=[VMEM] * 5,
        out_specs=HBM,
        scratch_shapes=[
            pltpu.VMEM((NC * PITCH, LANES), jnp.float32),
            pltpu.VMEM((M2 * PITCH, LANES), jnp.float32),
            pltpu.VMEM((NC, ROWS, LANES), jnp.float32),
            pltpu.SemaphoreType.DMA((2,)),
        ],
        compiler_params=pltpu.CompilerParams(vmem_limit_bytes=16 << 20),
        name="speciate",
    )(*[on_chip(v) for v in tabs], on_chip(total))


def shards(totals, courant, diffusion, stoich, log_k, mineral_stoich, mineral_log_k,
           mineral_rate, front_counts, mineral_flags):
    count = lax.axis_size("wide")
    pairs = [(i, i ^ 1) for i in range(count)]
    across = [(i, ((i + 1) ^ 1) - 1) for i in range(1, count - 1)]
    to_pair, to_next = pack(totals, courant, diffusion)
    nxt = lax.ppermute(to_next, "wide", across)
    pair = lax.ppermute(to_pair, "wide", pairs)
    moved = transport(pair, nxt, totals, courant, diffusion)
    total = lax.all_to_all(moved, "narrow", split_axis=0, concat_axis=0)
    tabs = tables(stoich.T, mineral_stoich, log_k.reshape(1, NSEC), mineral_log_k.reshape(1, NM), mineral_rate.reshape(1, NM),
                  front_counts.T, mineral_flags.reshape(NBLK))
    return speciate(tabs, total.reshape(NC * ROWS, LANES))


def solution(mesh):
    placed = (
        P("narrow", "wide", None), P("wide", None), P("wide", None),
        P(), P(), P(), P(), P(), P(), P("wide", "narrow"),
    )
    return jax.shard_map(
        shards, mesh=mesh, in_specs=placed, out_specs=P(None, "wide", "narrow"), check_vma=False
    )
```

```python
import functools

import jax
import jax.numpy as jnp
from jax import lax
from jax.experimental import pallas as pl
from jax.experimental.pallas import tpu as pltpu
from jax.sharding import PartitionSpec as P


STEPS = 4
ITERS = 4
HALO = 4
EARLY, LATE = 4, 2
NC = 16
ROWS = 32
LANES = 128
NBLK = 16
NSEC = 32
NM = 12
KS = 48
OFF = -16384.0
PITCH = 9
LOG2E = 1.4426950408889634
LN2 = 0.6931471805599453
PAIRS = [(i, j) for i in range(NC) for j in range(i, NC)]
PIDX = {p: n for n, p in enumerate(PAIRS)}
NP = len(PAIRS)
M2 = NP + NC
HBM = pl.BlockSpec(memory_space=pl.ANY)
VMEM = pl.BlockSpec(memory_space=pltpu.VMEM)


def on_chip(x):
    return pltpu.with_memory_space_constraint(x, pltpu.VMEM)


def in_hbm(x):
    return pltpu.with_memory_space_constraint(x, pltpu.HBM)


def vmem_out(shape, dtype=jnp.float32):
    return pltpu.VMEM(shape, dtype)


def split2(v):
    hi = v.astype(jnp.bfloat16)
    lo = (v - hi.astype(jnp.float32)).astype(jnp.bfloat16)
    return hi, lo


def is_even():
    return lax.rem(lax.axis_index("wide"), 2) == 0


def pack_kernel(tot_ref, cour_ref, diff_ref, pair_ref, next_ref, edge_ref, sems):
    copies = []
    for side, start in enumerate((0, ROWS - 8)):
        for n, (src, dst) in enumerate((
            (tot_ref.at[:, start:start + 8, :], edge_ref.at[side, 0:4]),
            (cour_ref.at[start:start + 8, :], edge_ref.at[side, 4]),
            (diff_ref.at[start:start + 8, :], edge_ref.at[side, 5]),
        )):
            copies.append(pltpu.make_async_copy(src, dst, sems.at[3 * side + n]))
    for c in copies:
        c.start()
    for c in copies:
        c.wait()
    first = edge_ref[0, :, 0:HALO, :]
    last = edge_ref[1, :, 8 - HALO:8, :]
    even = is_even()
    pair_ref[...] = jnp.where(even, last, first)
    next_ref[...] = jnp.where(even, first, last)


def pack(totals, courant, diffusion):
    width = totals.shape[2]
    return pl.pallas_call(
        pack_kernel,
        out_shape=[vmem_out((6, HALO, width))] * 2,
        in_specs=[HBM] * 3,
        out_specs=[VMEM] * 2,
        scratch_shapes=[pltpu.VMEM((2, 6, 8, width), jnp.float32), pltpu.SemaphoreType.DMA((6,))],
        compiler_params=pltpu.CompilerParams(vmem_limit_bytes=4 << 20),
        name="pack",
    )(*[in_hbm(v) for v in (totals, courant, diffusion)])


def transport_kernel(pair_ref, next_ref, tot_ref, cour_ref, diff_ref, out_ref, buf_ref, coef_ref, res_ref, sems):
    tiles = buf_ref.shape[2]
    even = is_even()
    parts = [slice(k * LANES, (k + 1) * LANES) for k in range(tiles)]
    zeros = jnp.zeros((8, LANES), jnp.float32)
    for slot in range(2):
        for c in range(4):
            for k in range(tiles):
                buf_ref[slot, c, k, 0:8, :] = zeros
                buf_ref[slot, c, k, 48:56, :] = zeros

    def extend(dst, own, part):
        before = jnp.where(even, next_ref[part], pair_ref[part])
        after = jnp.where(even, pair_ref[part], next_ref[part])
        for k, cols in enumerate(parts):
            dst[k, 8:12, :] = before[:, cols]
            dst[k, 12:44, :] = own[:, cols]
            dst[k, 44:48, :] = after[:, cols]

    extend(coef_ref.at[0], cour_ref[...], 4)
    extend(coef_ref.at[1], diff_ref[...], 5)
    mid = slice(8, 48)
    for k in range(tiles):
        u, d = coef_ref[0, k, mid, :], coef_ref[1, k, mid, :]
        coef_ref[2, k, mid, :] = 1.0 - u - 4.0 * d
        coef_ref[0, k, mid, :] = u + d
    for c in range(4):
        extend(buf_ref.at[0, c], tot_ref[c], c)
    copies = []

    def advance(step, c):
        src, dst = step % 2, (step + 1) % 2
        last = step == STEPS - 1
        lo, hi = (12, 44) if last else (8, 48)
        rows = slice(lo, hi)
        lane = lax.broadcasted_iota(jnp.int32, (hi - lo, LANES), 1)
        f = [buf_ref[src, c, k, rows, :] for k in range(tiles)]
        right = [pltpu.roll(v, 1, 1) for v in f]
        left = [pltpu.roll(v, LANES - 1, 1) for v in f]
        for k in range(tiles):
            west = jnp.where(lane == 0, right[k - 1] if k else 0.0, right[k])
            east = jnp.where(lane == LANES - 1, left[k + 1] if k + 1 < tiles else 0.0, left[k])
            up = buf_ref[src, c, k, lo - 1:hi - 1, :]
            down = buf_ref[src, c, k, lo + 1:hi + 1, :]
            new = coef_ref[2, k, rows, :] * f[k] + coef_ref[0, k, rows, :] * up
            new = new + coef_ref[1, k, rows, :] * (down + (west + east))
            if last:
                res_ref[k, c * ROWS:(c + 1) * ROWS, :] = new
            else:
                buf_ref[dst, c, k, rows, :] = new
        if last:
            own = slice(c * ROWS, (c + 1) * ROWS)
            copies.append(pltpu.make_async_copy(res_ref.at[:, own, :], out_ref.at[:, own, :], sems.at[c]))
            copies[-1].start()

    for step in range(STEPS):
        for c in range(4):
            advance(step, c)
    for c in copies:
        c.wait()


def transport(pair, nxt, totals, courant, diffusion):
    tiles = totals.shape[2] // LANES
    return pl.pallas_call(
        transport_kernel,
        out_shape=jax.ShapeDtypeStruct((4, 4 * ROWS, LANES), jnp.float32),
        in_specs=[VMEM] * 5,
        out_specs=HBM,
        scratch_shapes=[
            pltpu.VMEM((2, 4, tiles, 56, LANES), jnp.float32),
            pltpu.VMEM((3, tiles, 56, LANES), jnp.float32),
            pltpu.VMEM((4, 4 * ROWS, LANES), jnp.float32),
            pltpu.SemaphoreType.DMA((4,)),
        ],
        compiler_params=pltpu.CompilerParams(vmem_limit_bytes=8 << 20),
        name="transport",
    )(*[on_chip(v) for v in (pair, nxt, totals, courant, diffusion)])


def tables_kernel(st_ref, ms_ref, lk_ref, mk_ref, mr_ref, counts_ref, flags_ref,
                  l1_ref, l2_ref, unit_ref, front_ref,
                  sq_ref, tab_ref, vec_ref, st, ms, lks, mks, mrs, cs, fs, sems):
    wide, narrow = lax.axis_index("wide"), lax.axis_index("narrow")
    copies = [pltpu.make_async_copy(src, dst, sems.at[n]) for n, (src, dst) in enumerate((
        (st_ref, st), (ms_ref, ms), (lk_ref, lks), (mk_ref, mks), (mr_ref, mrs), (counts_ref, cs), (flags_ref, fs)))]
    for c in copies:
        c.start()
    sq_ref[...] = jnp.zeros(sq_ref.shape, jnp.float32)
    vec_ref[...] = jnp.zeros(vec_ref.shape, jnp.float32)
    vec_ref[2:3, :] = jnp.ones((1, LANES), jnp.float32)
    for c in copies:
        c.wait()
    sq_ref[0, 0:NC, 0:NSEC] = st[...]
    sq_ref[1, NSEC:NSEC + NM, 0:NC] = ms[...]
    vec_ref[0:1, 0:NSEC] = lks[...]
    vec_ref[1:2, 0:NM] = mks[...]
    vec_ref[2:3, 0:NM] = mrs[...]
    at = sq_ref[0] + sq_ref[1].T
    vec = vec_ref[...]
    shifted = pltpu.roll(vec * -LOG2E, NSEC, 1)[1:2, :] + pltpu.roll(jnp.log(vec_ref[2:3, :]) * LOG2E, NSEC, 1)
    bias = vec[0:1, :] * LOG2E + shifted
    lane = lax.broadcasted_iota(jnp.int32, (1, LANES), 1)
    off = jnp.where((lane >= NSEC) & (lane < NSEC + NM), OFF, 0.0)
    hi, lo = split2(at[0:NC, :])
    b1, b2 = split2(bias)
    b3 = (bias - b1.astype(jnp.float32)) - b2.astype(jnp.float32)
    sq_ref[0, 0:NC, :] = hi.astype(jnp.float32)
    sq_ref[0, NC:2 * NC, :] = hi.astype(jnp.float32)
    sq_ref[0, 2 * NC:3 * NC, :] = lo.astype(jnp.float32)
    sq_ref[0, 48:49, :] = b1.astype(jnp.float32)
    sq_ref[0, 49:50, :] = b2.astype(jnp.float32)
    sq_ref[0, 50:51, :] = b3
    sq_ref[0, 51:52, :] = off
    l1_ref[...] = sq_ref[0].T[0:KS, 0:4 * NC].astype(jnp.bfloat16)
    row = 0
    for i in range(NC + 1):
        tab = at[i:NC, :] * at[i:i + 1, :] if i < NC else at[0:NC, :]
        n = tab.shape[0]
        tab_ref[row:row + n, :] = tab
        row += n
    hi, lo = split2(tab_ref[...])
    hi, lo = hi.astype(jnp.float32), lo.astype(jnp.float32)
    lo = pltpu.roll(lo, 2 * KS, 1)
    lane = lax.broadcasted_iota(jnp.int32, lo.shape, 1)
    l2_ref[:, 0:128] = jnp.where(lane < 2 * KS, hi + pltpu.roll(hi, KS, 1), lo).astype(jnp.bfloat16)
    l2_ref[:, 128:3 * KS] = lo[:, 0:3 * KS - 128].astype(jnp.bfloat16)
    row = lax.broadcasted_iota(jnp.int32, (16, LANES), 0)
    for b in range(NBLK):
        absent = 1.0 - fs[b].astype(jnp.float32)
        unit_ref[b] = jnp.where(row < 3, 1.0, jnp.where(row == 3, absent, 0.0)).astype(jnp.bfloat16)
    count = cs[narrow, wide]
    front_ref[...] = jnp.where(lax.broadcasted_iota(jnp.int32, (ROWS, LANES), 0) < 2 * count, 1.0, 0.0)


def tables(stoich, mineral_stoich, log_k, mineral_log_k, mineral_rate, counts, flags):
    return pl.pallas_call(
        tables_kernel,
        out_shape=[vmem_out((KS, 4 * NC), jnp.bfloat16), vmem_out((M2, 3 * KS), jnp.bfloat16),
                   vmem_out((NBLK, 16, LANES), jnp.bfloat16), vmem_out((ROWS, LANES))],
        in_specs=[HBM] * 7,
        out_specs=[VMEM] * 4,
        scratch_shapes=[
            pltpu.VMEM((2, 128, 128), jnp.float32), pltpu.VMEM((M2, 128), jnp.float32), pltpu.VMEM((8, LANES), jnp.float32),
            pltpu.VMEM((NC, NSEC), jnp.float32), pltpu.VMEM((NM, NC), jnp.float32),
            pltpu.VMEM((1, NSEC), jnp.float32), pltpu.VMEM((1, NM), jnp.float32), pltpu.VMEM((1, NM), jnp.float32),
            pltpu.SMEM(counts.shape, jnp.int32), pltpu.SMEM((NBLK,), jnp.int32),
            pltpu.SemaphoreType.DMA((7,)),
        ],
        compiler_params=pltpu.CompilerParams(vmem_limit_bytes=4 << 20),
        name="tables",
    )(*[in_hbm(v) for v in (stoich, mineral_stoich, log_k, mineral_log_k, mineral_rate, counts, flags)])


def speciate_kernel(l1_ref, l2_ref, unit_ref, front_ref, tot_ref, out_ref, res_ref, sems, *scratch):
    y_refs, jac_refs = scratch[:4], scratch[4:]
    for k in range(NC):
        start = jnp.log(tot_ref[k * ROWS:(k + 1) * ROWS, :])
        res_ref[k] = start
        for g, y_ref in enumerate(y_refs):
            y_ref[k * PITCH:k * PITCH + 8, :] = start[8 * g:8 * g + 8] * LOG2E
    l1 = l1_ref[...]
    l2 = l2_ref[...]

    def stage(groups):
        s, x = {}, {}
        for g in groups:
            rows = range(8 * g, 8 * g + 8)
            ys = jnp.concatenate([y_refs[g][pl.ds(r, NC, stride=PITCH), :] for r in range(8)], axis=1)
            unit = jnp.concatenate([unit_ref[r // 2] for r in rows], axis=1)
            y1, y2 = split2(ys)
            s[g] = jnp.dot(l1, jnp.concatenate([y1, y2, y1, unit], axis=0), preferred_element_type=jnp.float32)
            yield
        for g in groups:
            x1, x2 = split2(jnp.exp2(s[g]))
            x[g] = jnp.concatenate([x1, x2, x1], axis=0)
            yield
            gm = jnp.dot(l2, x[g], preferred_element_type=jnp.float32)
            for n in range(8):
                jac_refs[g][pl.ds(n, M2, stride=PITCH), :] = gm[:, n * LANES:(n + 1) * LANES]
            yield

    def solve(groups):
        def jac(p, g):
            return jac_refs[g][p * PITCH:p * PITCH + 8, :]

        def ysl(k):
            return slice(k * PITCH, k * PITCH + 8)

        w = {g: [[None] * NC for _ in range(NC + 1)] for g in groups}
        rd = {g: [None] * NC for g in groups}
        for j in range(NC):
            lj = {g: [w[g][j][k] * rd[g][k] for k in range(j)] for g in groups}
            for i in range(j, NC + 1):
                for g in groups:
                    if i == NC:
                        acc = jac(NP + j, g) + jnp.exp2(y_refs[g][ysl(j), :]) - tot_ref[j * ROWS + 8 * g:j * ROWS + 8 * g + 8, :]
                    else:
                        acc = jac(PIDX[(j, i)], g)
                        if i == j:
                            acc = acc + jnp.exp2(y_refs[g][ysl(j), :])
                    for k in range(j):
                        acc = acc - w[g][i][k] * lj[g][k]
                    w[g][i][j] = acc
                    if i == j:
                        rd[g][j] = 1.0 / acc
            yield
        sol = {g: [None] * NC for g in groups}
        for j in reversed(range(NC)):
            for g in groups:
                acc = w[g][NC][j]
                for i in reversed(range(j + 1, NC)):
                    acc = acc - w[g][i][j] * sol[g][i]
                sol[g][j] = acc * rd[g][j]
            yield
        for g in groups:
            largest = functools.reduce(jnp.maximum, [jnp.abs(v) for v in sol[g]])
            scale = LOG2E / jnp.maximum(largest, 1.0)
            for j in range(NC):
                y_refs[g][ysl(j), :] = y_refs[g][ysl(j), :] - sol[g][j] * scale
        yield

    def out_copy(half):
        rows = slice(16 * half, 16 * half + 16)
        return pltpu.make_async_copy(res_ref.at[:, rows, :], out_ref.at[:, rows, :], sems.at[half])

    def finish(half):
        rows = slice(16 * half, 16 * half + 16)
        front = front_ref[rows, :] > 0.5
        for k in range(NC):
            sol = jnp.concatenate([y_refs[g][k * PITCH:k * PITCH + 8, :] for g in halves[half]], axis=0) * LN2
            res_ref[k, rows, :] = jnp.where(front, sol, res_ref[k, rows, :])
        out_copy(half).start()

    def weave(*plans):
        slots = sorted((step / count, n) for n, (_, count) in enumerate(plans) for step in range(count))
        for _, n in slots:
            next(plans[n][0])

    halves = ((0, 1), (2, 3))
    pieces = 6
    both = front_ref[16, 0] > 0.5

    @pl.when(both)
    def _():
        weave((stage(halves[0]), pieces))
        now = solve(halves[0])
        weave((now, EARLY))
        for turn in range(2 * ITERS):
            half = turn % 2
            other = None
            if turn + 1 < 2 * ITERS:
                weave((now, NC - EARLY - LATE), (stage(halves[1 - half]), pieces))
                other = solve(halves[1 - half])
                weave((now, LATE + NC + 1), (other, EARLY))
            else:
                weave((now, NC - EARLY + NC + 1))
            if turn >= 2 * ITERS - 2:
                finish(half)
            now = other

    @pl.when(jnp.logical_not(both))
    def _():
        out_copy(1).start()

        def body(it, carry):
            weave((stage(halves[0]), pieces))
            weave((solve(halves[0]), 2 * NC + 1))
            return carry

        lax.fori_loop(0, ITERS, body, 0)
        finish(0)

    out_copy(0).wait()
    out_copy(1).wait()


def speciate(tabs, total):
    return pl.pallas_call(
        speciate_kernel,
        out_shape=jax.ShapeDtypeStruct((NC, ROWS, LANES), jnp.float32),
        in_specs=[VMEM] * 5,
        out_specs=HBM,
        scratch_shapes=[
            pltpu.VMEM((NC, ROWS, LANES), jnp.float32),
            pltpu.SemaphoreType.DMA((2,)),
            *[pltpu.VMEM((NC * PITCH, LANES), jnp.float32)] * 4,
            *[pltpu.VMEM((M2 * PITCH, LANES), jnp.float32)] * 4,
        ],
        compiler_params=pltpu.CompilerParams(vmem_limit_bytes=16 << 20),
        name="speciate",
    )(*[on_chip(v) for v in tabs], on_chip(total))


def shards(totals, courant, diffusion, stoich, log_k, mineral_stoich, mineral_log_k,
           mineral_rate, front_counts, mineral_flags):
    count = lax.axis_size("wide")
    pairs = [(i, i ^ 1) for i in range(count)]
    across = [(i, ((i + 1) ^ 1) - 1) for i in range(1, count - 1)]
    to_pair, to_next = pack(totals, courant, diffusion)
    nxt = lax.ppermute(to_next, "wide", across)
    pair = lax.ppermute(to_pair, "wide", pairs)
    moved = transport(pair, nxt, totals, courant, diffusion)
    total = lax.all_to_all(moved, "narrow", split_axis=0, concat_axis=0)
    tabs = tables(stoich.T, mineral_stoich, log_k.reshape(1, NSEC), mineral_log_k.reshape(1, NM), mineral_rate.reshape(1, NM),
                  front_counts.T, mineral_flags.reshape(NBLK))
    return speciate(tabs, total.reshape(NC * ROWS, LANES))


def solution(mesh):
    placed = (
        P("narrow", "wide", None), P("wide", None), P("wide", None),
        P(), P(), P(), P(), P(), P(), P("wide", "narrow"),
    )
    return jax.shard_map(
        shards, mesh=mesh, in_specs=placed, out_specs=P(None, "wide", "narrow"), check_vma=False
    )
```
